32 devices in a mesh: row: 4 (over y, core), col: 4 (over z), exp: 2 (over x).
Axes of the slice: x: 2, y: 2, z: 4, core: 2. Of those that a mesh axis runs over, the one named last changes fastest.
Arguments:
- tokens: bfloat16 [4096, 2048], P(('row', 'exp')), may hold values from -6 to 6
- attn_gain: bfloat16 [2048], P(('row', 'exp')), may hold values from 0.5 to 1.5
- query_proj: bfloat16 [2048, 3072], P(('row', 'exp'), 'col'), may hold values from -0.125 to 0.125
- latent_proj: bfloat16 [2048, 576], P(('row', 'exp'), 'col'), may hold values from -0.125 to 0.125
- latent_gain: bfloat16 [512], P(('row', 'exp')), may hold values from 0.5 to 1.5
- keyval_proj: bfloat16 [512, 4096], P(('row', 'exp'), 'col'), may hold values from -0.25 to 0.25
- output_proj: bfloat16 [2048, 2048], P('col', ('row', 'exp')), may hold values from -0.5 to 0.5
- mixer_gain: bfloat16 [2048], P(('row', 'exp')), may hold values from 0.5 to 1.5
- router_proj: bfloat16 [2048, 16], P(('row', 'exp')), may hold values from -0.046875 to 0.046875
- shared_gate: bfloat16 [2048, 2816], P(('row', 'exp'), 'col'), may hold values from -0.125 to 0.125
- shared_up: bfloat16 [2048, 2816], P(('row', 'exp'), 'col'), may hold values from -0.125 to 0.125
- shared_down: bfloat16 [2816, 2048], P('col', ('row', 'exp')), may hold values from -0.109375 to 0.109375
- expert_gate: bfloat16 [16, 2048, 1408], P(('row', 'exp'), None, 'col'), may hold values from -0.125 to 0.125
- expert_up: bfloat16 [16, 2048, 1408], P(('row', 'exp'), None, 'col'), may hold values from -0.125 to 0.125
- expert_down: bfloat16 [16, 1408, 2048], P(('row', 'exp'), 'col'), may hold values from -0.25 to 0.25
- routes: int32 [4096, 6], P(('row', 'exp')), may hold values from 0 to 15, all different within a row; in each aligned block of 512 rows (0 to 511, 512 to 1023, ...) at most 274 rows name the same one
- segments: int32 [8, 512], P(('row', 'exp')), may hold values from 0 to 1, never falling along the last dimension, each value on 1 to 384 neighbouring positions
- cotangent: bfloat16 [4096, 2048], P(('row', 'exp')), may hold values from -6 to 6
Outputs:
- layer_out: bfloat16 [4096, 2048], P(('row', 'exp'), 'col')
- tokens_grad: float32 [4096, 2048], P(('row', 'exp'))
- attn_gain_grad: float32 [2048], P(('row', 'exp'))
- query_grad: float32 [2048, 3072], P(('row', 'exp'), 'col')
- latent_grad: float32 [2048, 576], P(('row', 'exp'), 'col')
- latent_gain_grad: float32 [512], P(('row', 'exp'))
- keyval_grad: float32 [512, 4096], P(('row', 'exp'), 'col')
- output_grad: float32 [2048, 2048], P('col', ('row', 'exp'))
- mixer_gain_grad: float32 [2048], P(('row', 'exp'))
- router_grad: float32 [2048, 16], P(('row', 'exp'))
- shared_gate_grad: float32 [2048, 2816], P(('row', 'exp'), 'col')
- shared_up_grad: float32 [2048, 2816], P(('row', 'exp'), 'col')
- shared_down_grad: float32 [2816, 2048], P('col', ('row', 'exp'))
- expert_gate_grad: float32 [16, 2048, 1408], P(('row', 'exp'), None, 'col')
- expert_up_grad: float32 [16, 2048, 1408], P(('row', 'exp'), None, 'col')
- expert_down_grad: float32 [16, 1408, 2048], P(('row', 'exp'), 'col')
The draws below stay inside these ranges and needn't reach their ends.
Inputs may be any that keep to these rules, and one draw needn't show every extreme that they name: `routes`: each token names 6 different experts. Among the 512 tokens of one block at most 274 name the same expert, and that many do for some expert. `segments`: within each block the ids never fall; a document is one run of equal ids, of 128 to 384 tokens.
All inputs are finite; a program needn't handle non-finite values.
Results may differ from the reference program's by a relative error of at most 0.024.
Values may be sent and summed in bfloat16 or wider, within the bound.
No kernel may reach another device: no remote copies, remote signals or barrier semaphores. Data moves between devices by JAX's collectives and lax.ppermute only.
A program may use at most 384 MiB of HBM per device.

```python
import math
import jax
import jax.numpy as jnp
import numpy as np
from jax import lax

D = 2048
HEADS = 16
NOPE = 128
ROPE = 64
VDIM = 128
RANK = 512
MOE_FF = 1408
SHARED_FF = 2816
TOP = 6
TOK_DEV = 512
GROUPS = 8
TOKENS = 4096
EXPERTS = 16
CAP = 274


def levels(own_key, extent, cuts, least, top_value):
    level = 1.0
    for axis_at, blocks in cuts:
        heights = jax.random.uniform(jax.random.fold_in(jax.random.fold_in(own_key, 6), axis_at), (blocks,), jnp.float32, least / len(cuts), top_value / len(cuts))
        level = level * jnp.repeat(jnp.exp(heights), extent[axis_at] // blocks).reshape((-1,) + (1,) * (len(extent) - 1 - axis_at))
    return level


def length_profile(number_of, total, bound, lean):
    weights = [(1 << 20) // math.isqrt(rank ** lean) + 1 for rank in range(2, number_of + 1)]
    surplus, counts = total - bound - (number_of - 1), [1] * (number_of - 1)
    while surplus > 0:
        free = [i for i in range(number_of - 1) if counts[i] < bound]
        mass, left = sum([weights[i] for i in free]), surplus
        for i in free:
            extra = min(bound - counts[i], max(1, left * weights[i] // mass), surplus)
            counts[i] = counts[i] + extra
            surplus = surplus - extra
    return np.array([bound] + counts)


def ragged(own_key, count, total, reach, slope):
    if count == 2:
        one = jax.random.randint(own_key, (), max(1, total - reach), min(reach, total - 1) + 1)
        return jnp.stack([one, total - one])
    tallies = jnp.asarray(length_profile(count, total, reach, slope), jnp.int32)
    couples = (count - 1) // 2
    donor, sink = tallies[1:1 + 2 * couples:2], tallies[2:2 + 2 * couples:2]
    slack = jnp.minimum(donor - 1, reach - sink)
    moved = jax.random.randint(jax.random.fold_in(own_key, 1), (couples,), 0, 1 << 20) % (slack + 1)
    tallies = tallies.at[1:1 + 2 * couples:2].set(donor - moved).at[2:2 + 2 * couples:2].set(sink + moved)
    return tallies[jax.random.permutation(jax.random.fold_in(own_key, 2), count)]


def deal_out(stream_key, own, number, rows, number_of, top, reach, lean):
    sequence = jax.random.permutation(stream_key, number_of)
    heavy_load, ordinary = shares(number_of, rows * top, reach, lean, True), shares(number_of, rows * top, reach, lean, False)
    places = jnp.arange(number_of)

    def named(lengths, rotation):
        used = int((lengths > 0).sum())
        fixed = max(1, used // 4)
        passed = fixed + (places - fixed + rotation * (used - fixed)) % max(1, number_of - fixed)
        return jnp.zeros((number_of,), jnp.int32).at[sequence[jnp.where(places < fixed, places, passed)]].set(jnp.asarray(lengths, jnp.int32))

    lengths = jnp.where(number % 4 == 0, named(heavy_load, number // 4), named(ordinary, number - number // 4 - 1))
    mixed = jax.random.permutation(jax.random.fold_in(own, 3), number_of)
    source_of, sink = mixed[0:number_of // 2 * 2:2], mixed[1:number_of // 2 * 2:2]
    slack = jnp.minimum(lengths[source_of] - 1, reach - lengths[sink]) // 2
    slack = jnp.where((source_of == sequence[0]) | (sink == sequence[0]) | (lengths[sink] == 0), 0, jnp.maximum(slack, 0))
    passed = jax.random.randint(jax.random.fold_in(own, 4), (number_of // 2,), 0, 1 << 20) % (slack + 1)
    lengths = lengths.at[source_of].add(-passed).at[sink].add(passed)
    labels = jnp.searchsorted(jnp.cumsum(lengths), jnp.arange(rows * top), side="right").astype(jnp.int32)
    grid = labels.reshape(top, rows).T
    grid = grid[jax.random.permutation(jax.random.fold_in(own, 1), rows)]
    rotation = jax.random.randint(jax.random.fold_in(own, 2), (rows, 1), 0, top)
    return jnp.take_along_axis(grid, (jnp.arange(top)[None, :] + rotation) % top, axis=1)


def shares(amount, total, limit, lean, full):
    weights = [(1 << 20) // math.isqrt(grade ** lean) + 1 for grade in range(1, amount + 1)]
    largest = limit if full else min(limit, max(-(-total // amount), total * weights[0] // sum(weights)))
    least = 1 if total - largest >= amount - 1 else 0
    given, spare = [largest] + [least] * (amount - 1), total - largest - least * (amount - 1)
    while spare > 0:
        movable = [i for i in range(1, amount) if given[i] < largest] or [i for i in range(1, amount) if given[i] < limit]
        whole, budget = sum([weights[i] for i in movable]), spare
        for i in movable:
            extra = min(limit - given[i], max(1, budget * weights[i] // whole), spare)
            given[i] = given[i] + extra
            spare = spare - extra
    return np.array(given)


def gaussian(key, shape, width, most, cuts=(), kind=jnp.bfloat16):
    drawn = jax.random.normal(key, shape, jnp.float32) * width
    if len(cuts) > 0:
        drawn = levels(key, shape, cuts, -0.22, 0.18) * drawn
    return jnp.clip(drawn, min=-most, max=most).astype(kind)


def setup_inputs(seed: int = 0) -> dict:
    streams_of = jax.random.split(jax.random.key(seed), 19)
    tokens = gaussian(streams_of[0], (TOKENS, D), 1.0, 6.0, ((0, 8),))
    attn_gain = jnp.clip(1.0 + 0.1 * jax.random.normal(streams_of[1], (D,), jnp.float32), 0.5, 1.5).astype(jnp.bfloat16)
    query_proj = gaussian(streams_of[2], (D, HEADS * (NOPE + ROPE)), D ** -0.5, 0.125, ((0, 8), (1, 4)))
    latent_proj = gaussian(streams_of[3], (D, RANK + ROPE), D ** -0.5, 0.125, ((0, 8), (1, 4)))
    latent_gain = jnp.clip(1.0 + 0.1 * jax.random.normal(streams_of[4], (RANK,), jnp.float32), 0.5, 1.5).astype(jnp.bfloat16)
    keyval_proj = gaussian(streams_of[5], (RANK, HEADS * (NOPE + VDIM)), RANK ** -0.5, 0.25, ((0, 8), (1, 4)))
    output_proj = gaussian(streams_of[6], (HEADS * VDIM, D), (HEADS * VDIM // 16) ** -0.5, 0.5, ((0, 4), (1, 8)))
    mixer_gain = jnp.clip(1.0 + 0.1 * jax.random.normal(streams_of[7], (D,), jnp.float32), 0.5, 1.5).astype(jnp.bfloat16)
    router_proj = gaussian(streams_of[8], (D, EXPERTS), (9 * D) ** -0.5, 0.046875, ((0, 8),))
    shared_gate = gaussian(streams_of[9], (D, SHARED_FF), D ** -0.5, 0.125, ((0, 8), (1, 4)))
    shared_up = gaussian(streams_of[10], (D, SHARED_FF), D ** -0.5, 0.125, ((0, 8), (1, 4)))
    shared_down = gaussian(streams_of[11], (SHARED_FF, D), SHARED_FF ** -0.5, 0.109375, ((0, 4), (1, 8)))
    expert_gate = gaussian(streams_of[12], (EXPERTS, D, MOE_FF), D ** -0.5, 0.125, ((0, 8), (2, 4)))
    expert_up = gaussian(streams_of[13], (EXPERTS, D, MOE_FF), D ** -0.5, 0.125, ((0, 8), (2, 4)))
    expert_down = gaussian(streams_of[14], (EXPERTS, MOE_FF, D), (MOE_FF * TOP // EXPERTS) ** -0.5, 0.25, ((0, 8), (1, 4)))
    routes_keys = jax.random.split(jax.random.fold_in(streams_of[15], 1), TOKENS // TOK_DEV)
    routes_turns = jax.random.permutation(jax.random.fold_in(streams_of[15], 3), TOKENS // TOK_DEV)
    routes = jax.vmap(lambda own, number: deal_out(jax.random.fold_in(streams_of[15], 2), own, number, TOK_DEV, EXPERTS, TOP, CAP, 2))(routes_keys, routes_turns).reshape((TOKENS, TOP))
    segments = jax.vmap(lambda own: jnp.searchsorted(jnp.cumsum(ragged(own, 2, TOK_DEV, 3 * TOK_DEV // 4, 0)), jnp.arange(TOK_DEV), side="right"))(jax.random.split(streams_of[16], GROUPS)).reshape((GROUPS, TOK_DEV)).astype(jnp.int32)
    cotangent = gaussian(streams_of[17], (TOKENS, D), 1.0, 6.0, ((0, 8),))
    return {"tokens": tokens, "attn_gain": attn_gain, "query_proj": query_proj, "latent_proj": latent_proj, "latent_gain": latent_gain, "keyval_proj": keyval_proj, "output_proj": output_proj, "mixer_gain": mixer_gain, "router_proj": router_proj, "shared_gate": shared_gate, "shared_up": shared_up, "shared_down": shared_down, "expert_gate": expert_gate, "expert_up": expert_up, "expert_down": expert_down, "routes": routes, "segments": segments, "cotangent": cotangent}


EPS = 1e-06
ROUTE_SCALE = 2.446
ROPE_BASE = 50000.0

@jax.custom_vjp
def low(v):
    return lax.optimization_barrier(v.astype(jnp.bfloat16)).astype(jnp.float32)

@jax.custom_vjp
def low_back(v):
    return v

def low_keep(v):
    return (low(v), None)

def low_pass(kept, grad):
    return (grad,)

def back_keep(v):
    return (v, None)

def back_low(kept, grad):
    return (low(grad),)
low.defvjp(low_keep, low_pass)
low_back.defvjp(back_keep, back_low)

def highest(left, right):
    return jnp.dot(left, right, precision=lax.Precision.HIGHEST)

def rmsnorm(values, gain):
    return values * lax.rsqrt(lax.optimization_barrier(jnp.mean(values * values, axis=-1, keepdims=True)) + EPS) * gain

def swish(values):
    return values / (1.0 + jnp.exp(-values))

def rotary(values, cosine, sine):
    half = values.shape[-1] // 2
    first = values[..., :half]
    second = values[..., half:]
    return jnp.concatenate([first * cosine - second * sine, second * cosine + first * sine], axis=-1)

def block_attention(queries, keys_full, value_rows, seg_ids):
    scores = low_back(jnp.einsum('thd,shd->hts', queries, keys_full, precision=lax.Precision.HIGHEST))
    position = jnp.arange(seg_ids.shape[0], dtype=jnp.int32)
    allowed = (position[None, :] <= position[:, None]) & (seg_ids[:, None] == seg_ids[None, :])
    scores = jnp.where(allowed[None], scores, -1e+30)
    biggest = lax.optimization_barrier(jnp.max(scores, axis=-1, keepdims=True))
    expos = jnp.exp(scores - biggest)
    probs = expos / lax.optimization_barrier(jnp.sum(expos, axis=-1, keepdims=True))
    mixed = jnp.einsum('hts,shd->thd', low(probs), value_rows, precision=lax.Precision.HIGHEST)
    return low(low_back(mixed))

def forward(tokens, attn_gain, query_proj, latent_proj, latent_gain, keyval_proj, output_proj, mixer_gain, router_proj, shared_gate, shared_up, shared_down, expert_gate, expert_up, expert_down, routes, segments):
    scale = (NOPE + ROPE) ** (-0.5)
    position = (jnp.arange(TOKENS, dtype=jnp.int32) % TOK_DEV).astype(jnp.float32)
    freqs = ROPE_BASE ** (-jnp.arange(ROPE // 2, dtype=jnp.int32).astype(jnp.float32) * 2.0 / ROPE)
    angles = position[:, None] * freqs[None, :]
    cosine = jnp.cos(angles)
    sine = jnp.sin(angles)
    normed_in = low(rmsnorm(tokens, attn_gain))
    query_raw = low_back(highest(normed_in, query_proj)).reshape(TOKENS, HEADS, NOPE + ROPE)
    queries = low(jnp.concatenate([query_raw[..., :NOPE], rotary(query_raw[..., NOPE:], cosine[:, None], sine[:, None])], axis=-1) * scale)
    latent = low(low_back(highest(normed_in, latent_proj)))
    latent_norm = low(rmsnorm(latent[:, :RANK], latent_gain))
    key_rope = rotary(latent[:, RANK:], cosine, sine)
    keyval = low_back(highest(latent_norm, keyval_proj)).reshape(TOKENS, HEADS, NOPE + VDIM)
    keys_full = low(jnp.concatenate([keyval[..., :NOPE], jnp.broadcast_to(key_rope[:, None, :], (TOKENS, HEADS, ROPE))], axis=-1))
    value_rows = low(keyval[..., NOPE:])
    attended = lax.map(jax.checkpoint(lambda parts: block_attention(parts[0], parts[1], parts[2], parts[3])), (queries.reshape(GROUPS, TOK_DEV, HEADS, NOPE + ROPE), keys_full.reshape(GROUPS, TOK_DEV, HEADS, NOPE + ROPE), value_rows.reshape(GROUPS, TOK_DEV, HEADS, VDIM), segments))
    hidden_sum = tokens + low_back(highest(attended.reshape(TOKENS, HEADS * VDIM), output_proj))
    normed_mid = low(rmsnorm(hidden_sum, mixer_gain))
    logits = low_back(highest(normed_mid, router_proj))
    expos = jnp.exp(logits - lax.optimization_barrier(jnp.max(logits, axis=-1, keepdims=True)))
    router_prob = expos / lax.optimization_barrier(jnp.sum(expos, axis=-1, keepdims=True))
    route_weight = ROUTE_SCALE * jnp.take_along_axis(router_prob, routes, axis=1)
    shared_hidden = low(swish(low_back(highest(normed_mid, shared_gate))) * low_back(highest(normed_mid, shared_up)))
    shared_out = highest(shared_hidden, shared_down)
    flat_routes = routes.reshape(-1)
    padded_rows = jnp.concatenate([normed_mid, jnp.zeros((1, D), jnp.float32)], axis=0)
    padded_weight = jnp.concatenate([route_weight.reshape(-1), jnp.zeros((1,), jnp.float32)], axis=0)

    def expert_step(total, expert):
        picks = jnp.nonzero(flat_routes == expert, size=GROUPS * CAP, fill_value=TOKENS * TOP)[0]
        owners = picks // TOP
        rows_in = low_back(padded_rows[owners])
        gate_val = low_back(highest(rows_in, expert_gate[expert]))
        up_val = low_back(highest(rows_in, expert_up[expert]))
        inner = low(swish(gate_val) * up_val)
        result = low_back(low(highest(inner, expert_down[expert])))
        return (total.at[owners].add(padded_weight[picks][:, None] * result), None)
    routed, unused = lax.scan(jax.checkpoint(expert_step), jnp.zeros((TOKENS + 1, D), jnp.float32), jnp.arange(EXPERTS, dtype=jnp.int32))
    return hidden_sum + shared_out + routed[:TOKENS]

def reference(tokens, attn_gain, query_proj, latent_proj, latent_gain, keyval_proj, output_proj, mixer_gain, router_proj, shared_gate, shared_up, shared_down, expert_gate, expert_up, expert_down, routes, segments, cotangent):
    params = (tokens, attn_gain, query_proj, latent_proj, latent_gain, keyval_proj, output_proj, mixer_gain, router_proj, shared_gate, shared_up, shared_down, expert_gate, expert_up, expert_down)
    floats = [item.astype(jnp.float32) for item in params]

    def closed(*inputs):
        return forward(*inputs, routes, segments)
    layer, pullback = jax.vjp(closed, *floats)
    grads = pullback(cotangent.astype(jnp.float32))
    return (layer.astype(jnp.bfloat16), grads[0], grads[1], grads[2], grads[3], grads[4], grads[5], grads[6], grads[7], grads[8], grads[9], grads[10], grads[11], grads[12], grads[13], grads[14])
```

```python
import jax
import jax.numpy as jnp
from jax import lax
from jax.sharding import PartitionSpec as P

NOPE = 128
ROPE = 64
VDIM = 128
RANK = 512
TOP = 6
EPS = 1e-06
ROUTE_SCALE = 2.446
ROPE_BASE = 50000.0
BLOCKS = ("row", "exp")
LANES = 128
BF16 = jnp.bfloat16
F32 = jnp.float32


def matmul(left, right):
    return jnp.dot(left, right, preferred_element_type=F32)


def matmul_nt(left, right):
    return lax.dot_general(left, right, (((1,), (1,)), ((), ())), preferred_element_type=F32)


def matmul_tn(left, right):
    return lax.dot_general(left, right, (((0,), (0,)), ((), ())), preferred_element_type=F32)


def gather(values, axes, axis=0):
    return lax.all_gather(values, axes, axis=axis, tiled=True)


def scatter_sum(values, axes, axis=0):
    return lax.psum_scatter(values, axes, scatter_dimension=axis, tiled=True)


def rotary_tables(length, width):
    freqs = ROPE_BASE ** (
        -jnp.arange(width // 2, dtype=jnp.int32).astype(F32) * 2.0 / width
    )
    angles = jnp.arange(length, dtype=jnp.int32).astype(F32)[:, None] * freqs[None, :]
    return (jnp.cos(angles), jnp.sin(angles))


def rotary(values, cosine, sine):
    half = values.shape[-1] // 2
    first = values[..., :half]
    second = values[..., half:]
    return jnp.concatenate(
        [first * cosine - second * sine, second * cosine + first * sine], axis=-1
    )


def rotary_back(grads, cosine, sine):
    half = grads.shape[-1] // 2
    first = grads[..., :half]
    second = grads[..., half:]
    return jnp.concatenate(
        [first * cosine + second * sine, second * cosine - first * sine], axis=-1
    )


def swish_parts(values):
    sigma = 1.0 / (1.0 + jnp.exp(-values))
    return (values * sigma, sigma * (1.0 + values * (1.0 - sigma)))


def norm_back(grad_out, normed_hat, inverse, gain):
    scaled = gain * grad_out
    return inverse * (scaled - normed_hat * jnp.mean(scaled * normed_hat, axis=-1, keepdims=True))


def masked_scores(queries, keys_full, allowed):
    scores = jnp.einsum("thd,shd->hts", queries, keys_full, preferred_element_type=F32)
    return jnp.where(allowed[None], scores, -1e30)


def fill_slots(values, slot_index, count):
    return jnp.zeros((count + 1, values.shape[1]), values.dtype).at[slot_index].set(values)[:count]


def softmax_rows(logits):
    expos = jnp.exp(logits - jnp.max(logits, axis=-1, keepdims=True))
    return expos / jnp.sum(expos, axis=-1, keepdims=True)


def pad_rows(vector):
    rows = -(-vector.shape[0] // LANES)
    return jnp.pad(vector, (0, rows * LANES - vector.shape[0])).reshape(rows, LANES)


def pack_small(vectors):
    return jnp.concatenate([pad_rows(v.reshape(-1)) for v in vectors], axis=0)


def unpack_small(packed, groups, sizes):
    out, at = [], 0
    for size in sizes:
        rows = -(-size // LANES)
        piece = packed[:, at : at + rows].reshape(groups, rows * LANES)[:, :size]
        out.append(piece.reshape(-1))
        at += rows
    return out


def expert_columns(weights, wide):
    hidden = weights.shape[2]
    padded = jnp.pad(weights, ((0, 0), (0, 0), (0, wide - hidden)))
    return jnp.concatenate([padded[e] for e in range(weights.shape[0])], axis=1)


def dense_experts(rows_own, cot_all, member_all, router_full, expert_gate, expert_up, expert_down):
    owned, width, hidden = expert_gate.shape
    wide = -(-hidden // LANES) * LANES
    first = lax.axis_index(BLOCKS) * owned
    rows = gather(rows_own, BLOCKS)
    prob = softmax_rows(matmul(rows, router_full))
    weight = ROUTE_SCALE * jnp.where(member_all, prob, 0.0)
    weight = lax.dynamic_slice_in_dim(weight, first, owned, 1)
    member = lax.dynamic_slice_in_dim(member_all, first, owned, 1)
    spread = jnp.concatenate(
        [jnp.broadcast_to(weight[:, e : e + 1], (rows.shape[0], wide)) for e in range(owned)],
        axis=1,
    )
    gate_cols, up_cols = expert_columns(expert_gate, wide), expert_columns(expert_up, wide)
    down_rows = jnp.pad(expert_down, ((0, 0), (0, wide - hidden), (0, 0))).reshape(
        owned * wide, width
    )
    gate_val = matmul(rows, gate_cols)
    up_val = matmul(rows, up_cols)
    act, slope = swish_parts(gate_val)
    inner = (act * up_val).astype(BF16).astype(F32)
    inner_low = (inner * spread).astype(BF16)
    back = matmul_nt(cot_all, down_rows)
    products = jnp.sum((inner * back).reshape(-1, owned, wide), axis=-1)
    products = jnp.where(member, products, 0.0)
    inner_grad = back * spread
    both_grad = jnp.concatenate(
        [(inner_grad * up_val * slope).astype(BF16), (inner_grad * act).astype(BF16)], axis=1
    )
    out_part = matmul(inner_low, down_rows).astype(BF16)
    rows_part = matmul_nt(both_grad, jnp.concatenate([gate_cols, up_cols], axis=1)).astype(BF16)
    both_w = matmul_tn(rows, both_grad)
    down_w = matmul_tn(inner_low, cot_all)
    cut = lambda e, which: both_w[:, (which * owned + e) * wide :][:, :hidden]
    gate_w = jnp.stack([cut(e, 0) for e in range(owned)])
    up_w = jnp.stack([cut(e, 1) for e in range(owned)])
    down_w = down_w.reshape(owned, wide, width)[:, :hidden]
    return out_part, rows_part, products, first, (gate_w, up_w, down_w)


def routed_experts(rows_own, cot, routes, weight, expert_gate, expert_up, expert_down, capacity):
    tok_rows, width = rows_own.shape
    owned = expert_gate.shape[0]
    experts_all = owned * lax.axis_size(BLOCKS)
    flat_routes = routes.reshape(-1)
    hits = (flat_routes[:, None] == jnp.arange(experts_all, dtype=jnp.int32)[None, :]).astype(
        jnp.int32
    )
    slot_in = jnp.sum(hits * (jnp.cumsum(hits, axis=0) - 1), axis=1)
    owner_rows = jnp.arange(tok_rows * TOP, dtype=jnp.int32) // TOP
    slot_index = flat_routes * capacity + slot_in
    slot_rows = experts_all * capacity
    send = lambda v: lax.all_to_all(
        fill_slots(v, slot_index, slot_rows).reshape(experts_all, capacity, width),
        BLOCKS,
        split_axis=0,
        concat_axis=1,
        tiled=True,
    )
    receive = lambda v: lax.all_to_all(v, BLOCKS, split_axis=1, concat_axis=0, tiled=True).reshape(
        slot_rows, -1
    )[slot_index].reshape(tok_rows, TOP, -1).astype(F32)
    rows = send(rows_own[owner_rows])
    gate_val = jnp.einsum("bvn,bnl->bvl", rows, expert_gate, preferred_element_type=F32)
    up_val = jnp.einsum("bvn,bnl->bvl", rows, expert_up, preferred_element_type=F32)
    act, slope = swish_parts(gate_val)
    inner = (act * up_val).astype(BF16)
    out_part = jnp.einsum("esf,efd->esd", inner, expert_down, preferred_element_type=F32)
    picked = receive(scatter_sum(out_part, "col", 2).astype(BF16))
    routed_own = jnp.sum(weight[:, :, None] * picked, axis=1)
    quarter = routed_own.shape[1]
    cot_own = lax.dynamic_slice_in_dim(cot, lax.axis_index("col") * quarter, quarter, 1)
    weight_grad = lax.psum(jnp.sum(cot_own.astype(F32)[:, None, :] * picked, axis=-1), "col")
    slot_grad = (weight.reshape(-1)[:, None] * cot.astype(F32)[owner_rows]).astype(BF16)
    arrived = send(slot_grad)
    inner_grad = jnp.einsum("esd,efd->esf", arrived, expert_down, preferred_element_type=F32)
    gate_grad = (inner_grad * up_val * slope).astype(BF16)
    up_grad = (inner_grad * act).astype(BF16)
    down_w = jnp.einsum("esf,esd->efd", inner, arrived, preferred_element_type=F32)
    gate_w = jnp.einsum("pli,plm->pim", rows, gate_grad, preferred_element_type=F32)
    up_w = jnp.einsum("pli,plm->pim", rows, up_grad, preferred_element_type=F32)
    rows_part = jnp.einsum(
        "wog,wcg->woc", gate_grad, expert_gate, preferred_element_type=F32
    ) + jnp.einsum("wog,wcg->woc", up_grad, expert_up, preferred_element_type=F32)
    back_own = jnp.sum(receive(scatter_sum(rows_part, "col", 2).astype(BF16)), axis=1)
    to_rows = lambda v: lax.all_to_all(v, "col", split_axis=0, concat_axis=1, tiled=True)
    return to_rows(routed_own), to_rows(back_own), weight_grad, (gate_w, up_w, down_w)


def local(
    tokens,
    attn_gain,
    query_proj,
    latent_proj,
    latent_gain,
    keyval_proj,
    output_proj,
    mixer_gain,
    router_proj,
    shared_gate,
    shared_up,
    shared_down,
    expert_gate,
    expert_up,
    expert_down,
    routes,
    segments,
    cotangent,
):
    groups = lax.axis_size(BLOCKS)
    columns = lax.axis_size("col")
    col_index = lax.axis_index("col")
    tok_rows, width = tokens.shape
    own_rows = tok_rows // columns
    own = lambda v: lax.dynamic_slice_in_dim(v, col_index * own_rows, own_rows, 0)
    experts_all = expert_gate.shape[0] * groups
    capacity = 10 * tok_rows * TOP // (7 * experts_all)
    dense = groups * tok_rows <= 2 * expert_gate.shape[0] * groups * capacity
    scale = (NOPE + ROPE) ** (-0.5)
    query_cols, latent_cols = query_proj.shape[1], latent_proj.shape[1]
    sizes = [attn_gain.size, latent_gain.size, mixer_gain.size, router_proj.size]

    in_full = gather(jnp.concatenate([query_proj, latent_proj], axis=1), BLOCKS)
    small = gather(pack_small([attn_gain, latent_gain, mixer_gain, router_proj]), BLOCKS)
    gain_in, gain_latent, gain_mid, router_full = unpack_small(
        small.reshape(groups, -1, LANES), groups, sizes
    )
    gainin_f, gainlat_f, gainmid_f = (g.astype(F32) for g in (gain_in, gain_latent, gain_mid))
    router_full = router_full.reshape(width, experts_all)
    keyval_full = gather(keyval_proj, BLOCKS)
    output_t = gather(output_proj.T, BLOCKS)
    chosen = routes[:, :, None] == jnp.arange(experts_all, dtype=jnp.int32)[None, None, :]
    member = jnp.any(chosen, axis=1)
    shgate_full = gather(shared_gate, BLOCKS)
    shup_full = gather(shared_up, BLOCKS)
    shdown_t = gather(shared_down.T, BLOCKS)
    if dense:
        member_all = gather(member.astype(BF16), BLOCKS) > 0
        cot_all = gather(cotangent, BLOCKS)

    heads_dev = query_cols // (NOPE + ROPE)
    cosine, sine = rotary_tables(tok_rows, ROPE)
    tokens_f = tokens.astype(F32)
    inverse_in = lax.rsqrt(jnp.mean(tokens_f * tokens_f, axis=-1, keepdims=True) + EPS)
    hat_in = tokens_f * inverse_in
    normed_in = (hat_in * gainin_f).astype(BF16)
    in_out = matmul(normed_in, in_full)
    query_raw = in_out[:, :query_cols].reshape(tok_rows, heads_dev, NOPE + ROPE)
    queries = (
        jnp.concatenate(
            [query_raw[..., :NOPE], rotary(query_raw[..., NOPE:], cosine[:, None], sine[:, None])],
            axis=-1,
        )
        * scale
    ).astype(BF16)
    latent_part = in_out[:, query_cols:].astype(BF16)
    latent = gather(latent_part, "col", 1).astype(F32)
    latent_rows = latent[:, :RANK]
    inverse_lat = lax.rsqrt(jnp.mean(latent_rows * latent_rows, axis=-1, keepdims=True) + EPS)
    hat_lat = latent_rows * inverse_lat
    latent_norm = (hat_lat * gainlat_f).astype(BF16)
    key_rope = rotary(latent[:, RANK:], cosine, sine)
    keyval = matmul(latent_norm, keyval_full).reshape(tok_rows, heads_dev, NOPE + VDIM)
    keys_full = jnp.concatenate(
        [keyval[..., :NOPE], jnp.broadcast_to(key_rope[:, None, :], (tok_rows, heads_dev, ROPE))],
        axis=-1,
    ).astype(BF16)
    value_rows = keyval[..., NOPE:].astype(BF16)
    position = jnp.arange(tok_rows, dtype=jnp.int32)
    seg_ids = segments[0]
    allowed = (position[None, :] <= position[:, None]) & (seg_ids[:, None] == seg_ids[None, :])
    scores = masked_scores(queries, keys_full, allowed)
    biggest = jnp.max(scores, axis=-1, keepdims=True)
    expos = jnp.exp(scores - biggest)
    probs = expos / jnp.sum(expos, axis=-1, keepdims=True)
    probs_low = probs.astype(BF16)
    attended = (
        jnp.einsum("hts,shd->thd", probs_low, value_rows, preferred_element_type=F32)
        .astype(BF16)
        .reshape(tok_rows, heads_dev * VDIM)
    )
    attn_rows = scatter_sum(matmul_nt(attended, output_t).astype(BF16), "col")
    hidden_rows = own(tokens).astype(F32) + attn_rows.astype(F32)
    inverse_mid = lax.rsqrt(jnp.mean(hidden_rows * hidden_rows, axis=-1, keepdims=True) + EPS)
    hat_mid = hidden_rows * inverse_mid
    normed_rows = (hat_mid * gainmid_f).astype(BF16)
    normed_mid = gather(normed_rows, "col")

    shgate_val = matmul(normed_mid, shgate_full)
    shup_val = matmul(normed_mid, shup_full)
    shact, shslope = swish_parts(shgate_val)
    shared_hidden = (shact * shup_val).astype(BF16)
    shared_part = matmul_nt(shared_hidden, shdown_t)
    shinner_grad = matmul(cotangent, shdown_t)
    shgate_grad = (shinner_grad * shup_val * shslope).astype(BF16)
    shup_grad = (shinner_grad * shact).astype(BF16)
    shared_mid = matmul_nt(shgate_grad, shgate_full) + matmul_nt(shup_grad, shup_full)

    router_prob = softmax_rows(matmul(normed_rows, router_full))
    if dense:
        out_part, rows_part, products, first, expert_grads = dense_experts(
            normed_mid, cot_all, member_all, router_full, expert_gate, expert_up, expert_down
        )
        back_rows = scatter_sum(
            (scatter_sum(rows_part, BLOCKS).astype(F32) + shared_mid).astype(BF16), "col"
        ).astype(F32)
        placed = lax.dynamic_update_slice_in_dim(
            jnp.zeros((groups * tok_rows, experts_all), F32), products, first, 1
        )
        prob_grad = ROUTE_SCALE * scatter_sum(scatter_sum(placed, BLOCKS), "col")
        out_rows = scatter_sum(
            (scatter_sum(out_part, BLOCKS).astype(F32) + shared_part).astype(BF16), "col"
        ).astype(F32)
    else:
        probs_all = softmax_rows(matmul(normed_mid, router_full))
        weight = ROUTE_SCALE * jnp.sum(jnp.where(chosen, probs_all[:, None, :], 0.0), axis=-1)
        routed_rows, routed_back, weight_grad, expert_grads = routed_experts(
            normed_mid,
            cotangent,
            routes,
            weight,
            expert_gate,
            expert_up,
            expert_down,
            capacity,
        )
        out_rows = scatter_sum(shared_part.astype(BF16), "col").astype(F32) + routed_rows
        back_rows = scatter_sum(shared_mid.astype(BF16), "col").astype(F32) + routed_back
        prob_grad = own(
            ROUTE_SCALE * jnp.sum(jnp.where(chosen, weight_grad[:, :, None], 0.0), axis=1)
        )
    layer_rows = (hidden_rows + out_rows).astype(BF16)
    layer_out = lax.all_to_all(layer_rows, "col", split_axis=1, concat_axis=0, tiled=True)

    logit_grad = (
        router_prob * (prob_grad - jnp.sum(router_prob * prob_grad, axis=-1, keepdims=True))
    ).astype(BF16)
    router_wgrad = matmul_tn(normed_rows, logit_grad)
    mid_grad = back_rows + matmul_nt(logit_grad, router_full)
    mixer_wgrad = jnp.sum(mid_grad * hat_mid, axis=0)
    hidden_grad = own(cotangent).astype(F32) + norm_back(mid_grad, hat_mid, inverse_mid, gainmid_f)
    hidden_low = gather(hidden_grad.astype(BF16), "col")

    attended_grad = matmul(hidden_low, output_t).astype(BF16).reshape(tok_rows, heads_dev, VDIM)
    prob_wgrad = jnp.einsum(
        "thd,shd->hts", attended_grad, value_rows, preferred_element_type=F32
    )
    score_grad = (
        probs * (prob_wgrad - jnp.sum(probs * prob_wgrad, axis=-1, keepdims=True))
    ).astype(BF16)
    value_grad = jnp.einsum(
        "hts,thd->shd", probs_low, attended_grad, preferred_element_type=F32
    )
    query_grad_full = (
        jnp.einsum("hts,shd->thd", score_grad, keys_full, preferred_element_type=F32) * scale
    )
    key_grad = jnp.einsum("hts,thd->shd", score_grad, queries, preferred_element_type=F32)
    query_raw_grad = (
        jnp.concatenate(
            [
                query_grad_full[..., :NOPE],
                rotary_back(query_grad_full[..., NOPE:], cosine[:, None], sine[:, None]),
            ],
            axis=-1,
        )
        .astype(BF16)
        .reshape(tok_rows, query_cols)
    )
    keyval_rows_grad = (
        jnp.concatenate([key_grad[..., :NOPE], value_grad], axis=-1)
        .astype(BF16)
        .reshape(tok_rows, heads_dev * (NOPE + VDIM))
    )
    latnorm_part = matmul_nt(keyval_rows_grad, keyval_full)
    rope_part = jnp.sum(key_grad[..., NOPE:], axis=1)
    lat_sum = lax.psum(
        jnp.concatenate([latnorm_part, rope_part], axis=1).astype(BF16), "col"
    ).astype(F32)
    latnorm_grad, rope_grad = lat_sum[:, :RANK], lat_sum[:, RANK:]
    latgain_wgrad = jnp.sum(own(latnorm_grad * hat_lat), axis=0)
    latent_rows_grad = jnp.concatenate(
        [
            norm_back(latnorm_grad, hat_lat, inverse_lat, gainlat_f),
            rotary_back(rope_grad, cosine, sine),
        ],
        axis=-1,
    ).astype(BF16)
    latent_own_grad = lax.dynamic_slice_in_dim(
        latent_rows_grad, col_index * latent_cols, latent_cols, 1
    )
    in_cols_grad = jnp.concatenate([query_raw_grad, latent_own_grad], axis=1)
    in_rows = scatter_sum(matmul_nt(in_cols_grad, in_full).astype(BF16), "col").astype(F32)
    gainin_wgrad = jnp.sum(in_rows * own(hat_in), axis=0)
    token_rows = hidden_grad + norm_back(in_rows, own(hat_in), own(inverse_in), gainin_f)
    tokens_grad = gather(token_rows.astype(BF16), "col").astype(F32)

    reduce = lambda v: scatter_sum(v.astype(BF16), BLOCKS).astype(F32)
    shared_gate_grad = reduce(matmul_tn(normed_mid, shgate_grad))
    shared_up_grad = reduce(matmul_tn(normed_mid, shup_grad))
    shared_down_grad = reduce(matmul_tn(cotangent, shared_hidden)).T
    output_grad = reduce(matmul_tn(hidden_low, attended)).T
    keyval_grad = reduce(matmul_tn(latent_norm, keyval_rows_grad))
    in_wgrad = reduce(matmul_tn(normed_in, in_cols_grad))
    query_grad, latent_grad = in_wgrad[:, :query_cols], in_wgrad[:, query_cols:]
    pieces = [gainin_wgrad, latgain_wgrad, mixer_wgrad, router_wgrad.reshape(-1)]
    packed = jnp.stack(
        [
            pack_small([p.reshape(groups, -1)[g].astype(BF16) for p in pieces])
            for g in range(groups)
        ]
    )
    summed = lax.psum(lax.psum_scatter(packed, BLOCKS, scatter_dimension=0), "col").astype(F32)
    attn_gain_grad, latent_gain_grad, mixer_gain_grad, router_grad = unpack_small(
        summed[None], 1, sizes
    )
    return (
        layer_out,
        tokens_grad,
        attn_gain_grad,
        query_grad,
        latent_grad,
        latent_gain_grad,
        keyval_grad,
        output_grad,
        mixer_gain_grad,
        router_grad.reshape(router_proj.shape),
        shared_gate_grad,
        shared_up_grad,
        shared_down_grad,
        *expert_grads,
    )


def solution(mesh):
    rows, cols = P(BLOCKS, None), P(BLOCKS, "col")
    vector, turned = P(BLOCKS), P("col", BLOCKS)
    tall, flat = P(BLOCKS, None, "col"), P(BLOCKS, "col", None)
    in_specs = (
        rows, vector, cols, cols, vector, cols, turned, vector, rows, cols, cols, turned,
        tall, tall, flat, rows, rows, rows,
    )
    out_specs = (
        cols, rows, vector, cols, cols, vector, cols, turned, vector, rows, cols, cols, turned,
        tall, tall, flat,
    )
    return jax.shard_map(local, mesh=mesh, in_specs=in_specs, out_specs=out_specs, check_vma=False)
```

```python
import functools

import jax
import jax.numpy as jnp
from jax import lax
from jax.experimental import pallas as pl
from jax.experimental.pallas import tpu as pltpu
from jax.sharding import PartitionSpec as P


NOPE = 128
ROPE = 64
VDIM = 128
RANK = 512
TOP = 6
EPS = 1e-06
ROUTE_SCALE = 2.446
ROPE_BASE = 50000.0
BLOCKS = ("row", "exp")
LANES = 128
BF16 = jnp.bfloat16
F32 = jnp.float32
NT = (((1,), (1,)), ((), ()))


def matmul(left, right):
    return jnp.dot(left, right, preferred_element_type=F32)


def matmul_nt(left, right):
    return lax.dot_general(left, right, (((1,), (1,)), ((), ())), preferred_element_type=F32)


def matmul_tn(left, right):
    return lax.dot_general(left, right, (((0,), (0,)), ((), ())), preferred_element_type=F32)


def gather(values, axes, axis=0):
    return lax.all_gather(values, axes, axis=axis, tiled=True)


def scatter_sum(values, axes, axis=0):
    return lax.psum_scatter(values, axes, scatter_dimension=axis, tiled=True)


def rotary_tables(length, width):
    freqs = ROPE_BASE ** (
        -jnp.arange(width // 2, dtype=jnp.int32).astype(F32) * 2.0 / width
    )
    angles = jnp.arange(length, dtype=jnp.int32).astype(F32)[:, None] * freqs[None, :]
    return (jnp.cos(angles), jnp.sin(angles))


def rotary(values, cosine, sine):
    half = values.shape[-1] // 2
    first = values[..., :half]
    second = values[..., half:]
    return jnp.concatenate(
        [first * cosine - second * sine, second * cosine + first * sine], axis=-1
    )


def rotary_back(grads, cosine, sine):
    half = grads.shape[-1] // 2
    first = grads[..., :half]
    second = grads[..., half:]
    return jnp.concatenate(
        [first * cosine + second * sine, second * cosine - first * sine], axis=-1
    )


def swish_parts(values):
    sigma = 1.0 / (1.0 + jnp.exp(-values))
    return (values * sigma, sigma * (1.0 + values * (1.0 - sigma)))


def norm_back(grad_out, normed_hat, inverse, gain):
    scaled = gain * grad_out
    return inverse * (scaled - normed_hat * jnp.mean(scaled * normed_hat, axis=-1, keepdims=True))


def masked_scores(queries, keys_full, allowed):
    scores = jnp.einsum("thd,shd->hts", queries, keys_full, preferred_element_type=F32)
    return jnp.where(allowed[None], scores, -1e30)


def fill_slots(values, slot_index, count):
    return jnp.zeros((count + 1, values.shape[1]), values.dtype).at[slot_index].set(values)[:count]


def softmax_rows(logits):
    expos = jnp.exp(logits - jnp.max(logits, axis=-1, keepdims=True))
    return expos / jnp.sum(expos, axis=-1, keepdims=True)


def swap(values, axis, bit):
    return lax.ppermute(values, axis, [(i, i ^ bit) for i in range(lax.axis_size(axis))])


def over_x(values):
    return swap(values, "exp", 1)


def over_y(values):
    return swap(values, "row", 2)


def over_core(values):
    return swap(values, "row", 1)


def total(values):
    for axis in ("exp", "row", "col"):
        bit = 1
        while bit < lax.axis_size(axis):
            values = values + swap(values, axis, bit)
            bit *= 2
    return values


def spread_sum(part, axis, dim=0):
    count, index = lax.axis_size(axis), lax.axis_index(axis)
    size = part.shape[dim] // count
    cut = lambda k: lax.dynamic_slice_in_dim(part, k * size, size, dim)
    out = cut(index).astype(F32)
    for bits in range(1, count):
        sent = swap(cut(index ^ bits).astype(BF16), axis, bits)
        out = out + sent.astype(F32)
    return out


def spread_gather(own, axis):
    count, index = lax.axis_size(axis), lax.axis_index(axis)
    pieces = [own] + [swap(own, axis, bits) for bits in range(1, count)]
    bit = 1
    while bit < count:
        flip = (index & bit) > 0
        pieces = [jnp.where(flip, pieces[k ^ bit], pieces[k]) for k in range(count)]
        bit *= 2
    return jnp.concatenate(pieces, axis=0)


CHUNKS = {
    "o": ((0, 0), (0, 1), (2, 0), (2, 1)),
    "n": ((1, 0), (4, 1), (3, 0), (6, 1)),
    "f": ((5, 0), (5, 1), (7, 0), (7, 1)),
    "s": ((4, 0), (1, 1), (6, 0), (3, 1)),
}


def spread_blocks(own):
    half = own.shape[0] // 2
    first, second = own[:half], own[half:]
    near = over_x(first), over_y(second)
    side = over_y(first), over_x(second)
    far = over_y(near[0]), over_x(near[1])
    chunks = {}
    for name, pair in zip(CHUNKS, ((first, second), near, far, side)):
        chunks[name] = [*pair, *(over_core(v) for v in pair)]
    return chunks


def collect_blocks(chunks):
    half = chunks["o"].shape[0] // 4
    merged = []
    for chunk in chunks.values():
        other = over_core(chunk[2 * half :])
        merged.append(chunk[: 2 * half].astype(F32) + other.astype(F32))
    own, near, far, side = merged
    near = over_x(near[:half].astype(BF16)), over_y(near[half:].astype(BF16))
    far = over_x(far[:half].astype(BF16)), over_y(far[half:].astype(BF16))
    first = (side[:half] + far[0].astype(F32)).astype(BF16)
    second = (side[half:] + far[1].astype(F32)).astype(BF16)
    side = over_y(first), over_x(second)
    near, side = jnp.concatenate(near, axis=0), jnp.concatenate(side, axis=0)
    return own + near.astype(F32) + side.astype(F32)


def expert_kernel(count, owned, hidden, experts_all, starts, router_start, chained, info, *refs):
    pieces, refs = refs[:count], refs[count:]
    (cot_ref, member_ref, *weights), refs = refs[:5], refs[5:]
    router, refs = (refs[0], refs[1:]) if owned else (None, refs)
    refs = refs[chained:]
    if owned:
        back_ref, out_ref, rows_ref, inner_ref, gate_grad_ref, up_grad_ref = refs[:6]
        refs = refs[6:]
    else:
        back_ref, out_ref, inner_ref, gate_grad_ref, up_grad_ref = refs[:5]
        rows_ref, refs = None, refs[5:]
    rows_buf, weight_buf, rows_sem, weight_sem = refs
    step = pl.program_id(0)
    units, padded = inner_ref.shape[1], weight_buf.shape[1]
    width = out_ref.shape[1]
    row_copies = [
        pltpu.make_async_copy(pieces[j], rows_buf.at[j], rows_sem.at[j]) for j in range(count)
    ]
    weight_copies = [
        pltpu.make_async_copy(
            weights[j].at[pl.ds(starts[j], units)],
            weight_buf.at[j, pl.ds(0, units)],
            weight_sem.at[j],
        )
        for j in range(3)
    ]
    if owned:
        router_copy = pltpu.make_async_copy(
            router.at[pl.ds(router_start, experts_all)],
            weight_buf.at[0, pl.ds(units, experts_all)],
            weight_sem.at[3],
        )
        weight_copies.append(router_copy)

    @pl.when(step == 0)
    def _():
        row_copies[0].start()
        for copy in weight_copies + row_copies[1:]:
            copy.start()
        if owned:
            used = units + experts_all
            weight_buf[0, used:] = jnp.zeros((padded - used, width), BF16)
            for j in (1, 2):
                weight_buf[j, units:] = jnp.zeros((padded - units, width), BF16)

    for j in range(count):
        pl.when(step == j)(row_copies[j].wait)
    rows = rows_buf[step]
    pl.when(step == 0)(weight_copies[0].wait)
    if owned:
        pl.when(step == 0)(router_copy.wait)
    gate_val = lax.dot_general(rows, weight_buf[0], NT, preferred_element_type=F32)
    pl.when(step == 0)(weight_copies[1].wait)
    up_val = lax.dot_general(rows, weight_buf[1], NT, preferred_element_type=F32)
    pl.when(step == 0)(weight_copies[2].wait)
    back = lax.dot_general(cot_ref[...], weight_buf[2], NT, preferred_element_type=F32)
    act, slope = swish_parts(gate_val)
    inner = (act * up_val).astype(BF16)
    if owned:
        first = info[count]
        at = units // LANES * LANES
        lane = lax.broadcasted_iota(jnp.int32, (1, LANES), 1)
        logits = gate_val[:, at : at + LANES]
        valid = (lane >= units - at) & (lane < units - at + experts_all)
        logits = jnp.where(valid, logits, -jnp.inf)
        expos = jnp.exp(logits - jnp.max(logits, axis=1, keepdims=True))
        prob = expos / jnp.sum(expos, axis=1, keepdims=True)
        member = member_ref[...].astype(F32)
        narrow = lax.broadcasted_iota(jnp.int32, (1, experts_all), 1)
        unit = lax.broadcasted_iota(jnp.int32, (1, padded), 1) // hidden
        product = inner.astype(F32) * back
        spread, sums = None, 0.0
        for e in range(owned):
            chosen = jnp.sum(jnp.where(narrow == first + e, member, 0.0), axis=1, keepdims=True)
            weight = ROUTE_SCALE * jnp.sum(
                jnp.where(lane == units - at + first + e, prob, 0.0), axis=1, keepdims=True
            )
            weight = jnp.where(chosen > 0, weight, 0.0)
            spread = weight if e == 0 else jnp.where(unit == e, weight, spread)
            total = jnp.sum(jnp.where(unit == e, product, 0.0), axis=1, keepdims=True)
            total = jnp.where(chosen > 0, total, 0.0)
            sums = jnp.where(lane == first + e, total, sums)
        back_ref[:, width:] = sums.astype(BF16)
        inner = (inner.astype(F32) * spread).astype(BF16)
        back = back * spread
        rows_ref[...] = rows
    gate_grad = (back * up_val * slope).astype(BF16)
    up_grad = (back * act).astype(BF16)
    inner_ref[...] = inner[:, :units]
    gate_grad_ref[...] = gate_grad[:, :units]
    up_grad_ref[...] = up_grad[:, :units]
    back_ref[:, :width] = (
        jnp.dot(gate_grad, weight_buf[0], preferred_element_type=F32)
        + jnp.dot(up_grad, weight_buf[1], preferred_element_type=F32)
    ).astype(BF16)
    out_ref[...] = jnp.dot(inner, weight_buf[2], preferred_element_type=F32).astype(BF16)


def run_experts(pieces, cot_all, member_all, weights, starts, router, blocks, first, owned, units, before=()):
    count, (half, width) = len(pieces), pieces[0].shape
    padded = -(-(units + (member_all.shape[1] if owned else 0)) // LANES) * LANES if owned else units
    rows_all, experts_all = cot_all.shape[0], member_all.shape[1]
    info = jnp.concatenate([blocks, first[None]]).astype(jnp.int32)
    anywhere = pl.BlockSpec(memory_space=pl.ANY)
    placed = lambda w: pl.BlockSpec((half, w), lambda j, info: (info[j], 0))
    side = LANES if owned else 0
    shape = lambda r, w: jax.ShapeDtypeStruct((r, w), BF16)
    absolute = [width] + ([width] if owned else []) + [units] * 3
    extra = [router[0]] if owned else []
    before = list(before)
    first_in = 1 + count + 5 + len(extra)
    return pl.pallas_call(
        functools.partial(
            expert_kernel,
            count,
            owned,
            units // max(owned, 1),
            experts_all,
            starts,
            router[1],
            len(before),
        ),
        out_shape=[shape(count * half, width + side)] + [shape(rows_all, w) for w in absolute],
        grid_spec=pltpu.PrefetchScalarGridSpec(
            num_scalar_prefetch=1,
            grid=(count,),
            in_specs=[anywhere] * count
            + [placed(width), placed(experts_all)]
            + [anywhere] * (3 + len(extra) + len(before)),
            out_specs=[pl.BlockSpec((half, width + side), lambda j, info: (j, 0))]
            + [placed(w) for w in absolute],
            scratch_shapes=[
                pltpu.VMEM((count, half, width), BF16),
                pltpu.VMEM((3, padded, width), BF16),
                pltpu.SemaphoreType.DMA((count,)),
                pltpu.SemaphoreType.DMA((4,)),
            ],
        ),
        input_output_aliases={first_in + k: 1 + k for k in range(len(before))},
        cost_estimate=pl.CostEstimate(
            flops=12 * count * half * width * padded,
            bytes_accessed=2 * (3 * padded * width + count * half * (5 * width + 3 * units)),
            transcendentals=count * half * padded,
        ),
        compiler_params=pltpu.CompilerParams(vmem_limit_bytes=56 << 20),
        name="experts",
    )(info, *pieces, cot_all, member_all, *weights, *extra, *before)


def dense_experts(rows_own, cot_all, member_all, router, expert_gate, expert_up, expert_down):
    owned, width, hidden = expert_gate.shape
    units = owned * hidden
    index = lax.axis_index(BLOCKS)
    weights = [
        expert_gate.transpose(0, 2, 1).reshape(units, width),
        expert_up.transpose(0, 2, 1).reshape(units, width),
        expert_down.reshape(units, width),
    ]
    backs, placed = {}, ()
    chunks = spread_blocks(rows_own)
    for name, places in CHUNKS.items():
        blocks = jnp.stack([(index ^ rel) * 2 + part for rel, part in places])
        backs[name], *placed = run_experts(
            chunks[name],
            cot_all,
            member_all,
            weights,
            (0, 0, 0),
            router,
            blocks,
            index * owned,
            owned,
            units,
            placed,
        )
    back_sum = collect_blocks(backs)
    out_all, rows_all, inner_all, gate_grad, up_grad = placed
    turn = lambda v: v.reshape(owned, hidden, width).transpose(0, 2, 1)
    gate_w = matmul_tn(gate_grad, rows_all)
    up_w = matmul_tn(up_grad, rows_all)
    down_w = matmul_tn(inner_all, cot_all)
    grads_w = turn(gate_w), turn(up_w), down_w.reshape(owned, hidden, width)
    return back_sum, out_all, grads_w


def routed_experts(rows_own, cot, routes, weight, expert_gate, expert_up, expert_down, capacity):
    tok_rows, width = rows_own.shape
    owned = expert_gate.shape[0]
    experts_all = owned * lax.axis_size(BLOCKS)
    flat_routes = routes.reshape(-1)
    hits = (flat_routes[:, None] == jnp.arange(experts_all, dtype=jnp.int32)[None, :]).astype(
        jnp.int32
    )
    slot_in = jnp.sum(hits * (jnp.cumsum(hits, axis=0) - 1), axis=1)
    owner_rows = jnp.arange(tok_rows * TOP, dtype=jnp.int32) // TOP
    slot_index = flat_routes * capacity + slot_in
    slot_rows = experts_all * capacity
    send = lambda v: lax.all_to_all(
        fill_slots(v, slot_index, slot_rows).reshape(experts_all, capacity, width),
        BLOCKS,
        split_axis=0,
        concat_axis=1,
        tiled=True,
    )
    receive = lambda v: lax.all_to_all(v, BLOCKS, split_axis=1, concat_axis=0, tiled=True).reshape(
        slot_rows, -1
    )[slot_index].reshape(tok_rows, TOP, -1).astype(F32)
    rows = send(rows_own[owner_rows])
    gate_val = jnp.einsum("bvn,bnl->bvl", rows, expert_gate, preferred_element_type=F32)
    up_val = jnp.einsum("bvn,bnl->bvl", rows, expert_up, preferred_element_type=F32)
    act, slope = swish_parts(gate_val)
    inner = (act * up_val).astype(BF16)
    out_part = jnp.einsum("esf,efd->esd", inner, expert_down, preferred_element_type=F32)
    picked = receive(scatter_sum(out_part, "col", 2).astype(BF16))
    routed_own = jnp.sum(weight[:, :, None] * picked, axis=1)
    quarter = routed_own.shape[1]
    cot_own = lax.dynamic_slice_in_dim(cot, lax.axis_index("col") * quarter, quarter, 1)
    weight_grad = lax.psum(jnp.sum(cot_own.astype(F32)[:, None, :] * picked, axis=-1), "col")
    slot_grad = (weight.reshape(-1)[:, None] * cot.astype(F32)[owner_rows]).astype(BF16)
    arrived = send(slot_grad)
    inner_grad = jnp.einsum("esd,efd->esf", arrived, expert_down, preferred_element_type=F32)
    gate_grad = (inner_grad * up_val * slope).astype(BF16)
    up_grad = (inner_grad * act).astype(BF16)
    down_w = jnp.einsum("esf,esd->efd", inner, arrived, preferred_element_type=F32)
    gate_w = jnp.einsum("pli,plm->pim", rows, gate_grad, preferred_element_type=F32)
    up_w = jnp.einsum("pli,plm->pim", rows, up_grad, preferred_element_type=F32)
    rows_part = jnp.einsum(
        "wog,wcg->woc", gate_grad, expert_gate, preferred_element_type=F32
    ) + jnp.einsum("wog,wcg->woc", up_grad, expert_up, preferred_element_type=F32)
    back_own = jnp.sum(receive(scatter_sum(rows_part, "col", 2).astype(BF16)), axis=1)
    back_rows = lax.all_to_all(back_own, "col", split_axis=0, concat_axis=1, tiled=True)
    return routed_own, back_rows, weight_grad, (gate_w, up_w, down_w)


def layer(
    tokens,
    attn_gain,
    query_proj,
    latent_proj,
    latent_gain,
    keyval_proj,
    output_proj,
    mixer_gain,
    router_proj,
    shared_gate,
    shared_up,
    shared_down,
    expert_gate,
    expert_up,
    expert_down,
    routes,
    segments,
    cotangent,
):
    groups = lax.axis_size(BLOCKS)
    columns = lax.axis_size("col")
    col_index = lax.axis_index("col")
    tok_rows, width = tokens.shape
    own_rows = tok_rows // columns
    own = lambda v: lax.dynamic_slice_in_dim(v, col_index * own_rows, own_rows, 0)
    experts_all = expert_gate.shape[0] * groups
    capacity = 10 * tok_rows * TOP // (7 * experts_all)
    dense = (
        groups * tok_rows <= 2 * expert_gate.shape[0] * groups * capacity
        and lax.axis_size("row") == 4
        and lax.axis_size("exp") == 2
    )
    scale = (NOPE + ROPE) ** (-0.5)
    query_cols, latent_cols = query_proj.shape[1], latent_proj.shape[1]
    in_cols = query_cols + latent_cols

    part = attn_gain.size
    lane = lambda v: jnp.pad(v, (0, part - v.size))[None]
    kv_rows, kv_cols = keyval_proj.shape
    keyval_split = keyval_proj.reshape(kv_rows, -1, part).transpose(1, 0, 2).reshape(-1, part)
    kv_end = in_cols + keyval_split.shape[0]
    router_start = kv_end + output_proj.shape[0]
    query_t = lax.optimization_barrier(query_proj.T)
    weights_own = jnp.concatenate(
        [
            query_t,
            latent_proj.T,
            keyval_split,
            output_proj,
            router_proj.T,
            lane(attn_gain),
            lane(mixer_gain),
            lane(latent_gain),
        ],
        axis=0,
    )
    weights = gather(weights_own, BLOCKS, 1)
    in_t, output_full = weights[:in_cols], weights[kv_end:router_start]
    keyval_full = (
        weights[in_cols:kv_end]
        .reshape(-1, kv_rows, groups, part)
        .transpose(2, 1, 0, 3)
        .reshape(groups * kv_rows, kv_cols)
    )
    router_t = weights[router_start : router_start + experts_all]
    gainin_f, gainmid_f, gainlat_f = weights[router_start + experts_all :].astype(F32)
    gainlat_f = gainlat_f.reshape(groups, -1)[:, : latent_gain.size].reshape(-1)
    chosen = routes[:, :, None] == jnp.arange(experts_all, dtype=jnp.int32)[None, None, :]
    member = jnp.any(chosen, axis=1).astype(BF16)
    shared_own = jnp.concatenate(
        [shared_gate.T, shared_up.T, shared_down, member.reshape(-1, part)], axis=0
    )
    shared_full = gather(shared_own, BLOCKS, 1)
    hidden_sh = shared_gate.shape[1]
    member_all = (
        shared_full[3 * hidden_sh :]
        .reshape(-1, groups, part)
        .transpose(1, 0, 2)
        .reshape(groups * tok_rows, experts_all)
    )
    if dense:
        cot_all = gather(cotangent, BLOCKS)

    heads_dev = query_cols // (NOPE + ROPE)
    cosine, sine = rotary_tables(tok_rows, ROPE)
    tokens_f = tokens.astype(F32)
    inverse_in = lax.rsqrt(jnp.mean(tokens_f * tokens_f, axis=-1, keepdims=True) + EPS)
    hat_in = tokens_f * inverse_in
    normed_in = (hat_in * gainin_f).astype(BF16)
    in_out = matmul_nt(normed_in, in_t)
    query_raw = in_out[:, :query_cols].reshape(tok_rows, heads_dev, NOPE + ROPE)
    queries = (
        jnp.concatenate(
            [query_raw[..., :NOPE], rotary(query_raw[..., NOPE:], cosine[:, None], sine[:, None])],
            axis=-1,
        )
        * scale
    ).astype(BF16)
    latent_part = in_out[:, query_cols:].astype(BF16)
    latent = spread_gather(latent_part.T, "col").T.astype(F32)
    latent_rows = latent[:, :RANK]
    inverse_lat = lax.rsqrt(jnp.mean(latent_rows * latent_rows, axis=-1, keepdims=True) + EPS)
    hat_lat = latent_rows * inverse_lat
    latent_norm = (hat_lat * gainlat_f).astype(BF16)
    key_rope = rotary(latent[:, RANK:], cosine, sine)
    keyval = matmul(latent_norm, keyval_full).reshape(tok_rows, heads_dev, NOPE + VDIM)
    keys_full = jnp.concatenate(
        [keyval[..., :NOPE], jnp.broadcast_to(key_rope[:, None, :], (tok_rows, heads_dev, ROPE))],
        axis=-1,
    ).astype(BF16)
    value_rows = keyval[..., NOPE:].astype(BF16)
    position = jnp.arange(tok_rows, dtype=jnp.int32)
    seg_ids = segments[0]
    allowed = (position[None, :] <= position[:, None]) & (seg_ids[:, None] == seg_ids[None, :])
    scores = masked_scores(queries, keys_full, allowed)
    biggest = jnp.max(scores, axis=-1, keepdims=True)
    expos = jnp.exp(scores - biggest)
    probs = expos / jnp.sum(expos, axis=-1, keepdims=True)
    probs_low = probs.astype(BF16)
    attended = (
        jnp.einsum("hts,shd->thd", probs_low, value_rows, preferred_element_type=F32)
        .astype(BF16)
        .reshape(tok_rows, heads_dev * VDIM)
    )
    attn_rows = spread_sum(matmul(attended, output_full), "col")
    hidden_rows = own(tokens).astype(F32) + attn_rows
    inverse_mid = lax.rsqrt(jnp.mean(hidden_rows * hidden_rows, axis=-1, keepdims=True) + EPS)
    hat_mid = hidden_rows * inverse_mid
    normed_rows = (hat_mid * gainmid_f).astype(BF16)
    normed_mid = spread_gather(normed_rows, "col")

    if dense:
        half = tok_rows // 2
        shared_mid, shared_part, shared_hidden, shgate_grad, shup_grad = run_experts(
            [normed_mid[:half], normed_mid[half:]],
            cotangent,
            member,
            [shared_full] * 3,
            (0, hidden_sh, 2 * hidden_sh),
            (shared_full, 0),
            jnp.arange(2, dtype=jnp.int32),
            jnp.int32(0),
            0,
            hidden_sh,
        )
    else:
        shgate_t = shared_full[:hidden_sh]
        shup_t = shared_full[hidden_sh : 2 * hidden_sh]
        shdown_full = shared_full[2 * hidden_sh : 3 * hidden_sh]
        shup_val = matmul_nt(normed_mid, shup_t)
        shact, shslope = swish_parts(matmul_nt(normed_mid, shgate_t))
        shared_hidden = (shact * shup_val).astype(BF16)
        shared_part = matmul(shared_hidden, shdown_full)
        shinner_grad = matmul_nt(cotangent, shdown_full)
        shgate_grad = (shinner_grad * shup_val * shslope).astype(BF16)
        shup_grad = (shinner_grad * shact).astype(BF16)
        shared_mid = matmul(shgate_grad, shgate_t) + matmul(shup_grad, shup_t)

    reduce = lambda v, axis: scatter_sum(v.astype(BF16), BLOCKS, axis)
    shared_wgrad = [
        matmul_tn(shgate_grad, normed_mid),
        matmul_tn(shup_grad, normed_mid),
        matmul_tn(shared_hidden, cotangent),
    ]
    shared_wgrad = jnp.concatenate([v.astype(BF16) for v in shared_wgrad], axis=0)
    shared_wgrad = reduce(shared_wgrad, 1)
    hidden_cols, shared_mid = lax.optimization_barrier((hidden_rows.astype(BF16), shared_mid))
    hidden_cols = lax.all_to_all(hidden_cols, "col", split_axis=1, concat_axis=0, tiled=True)

    router_prob = softmax_rows(matmul_nt(normed_rows, router_t))
    if dense:
        back_sum, out_all, expert_grads = dense_experts(
            normed_mid,
            cot_all,
            member_all,
            (weights, router_start),
            expert_gate,
            expert_up,
            expert_down,
        )
        out_sum = scatter_sum(out_all, BLOCKS)
        out_sum = out_sum.astype(F32) + shared_part.astype(F32)
        back_sum = jnp.concatenate(
            [back_sum[:, :width] + shared_mid.astype(F32), back_sum[:, width:]], axis=1
        )
        back_rows = spread_sum(back_sum, "col")
        prob_grad = ROUTE_SCALE * back_rows[:, width : width + experts_all]
        back_rows = back_rows[:, :width]
    else:
        probs_all = softmax_rows(matmul_nt(normed_mid, router_t))
        weight = ROUTE_SCALE * jnp.sum(jnp.where(chosen, probs_all[:, None, :], 0.0), axis=-1)
        routed_own, routed_back, weight_grad, expert_grads = routed_experts(
            normed_mid,
            cotangent,
            routes,
            weight,
            expert_gate,
            expert_up,
            expert_down,
            capacity,
        )
        out_sum = shared_part
        back_rows = spread_sum(shared_mid, "col") + routed_back
        prob_grad = own(
            ROUTE_SCALE * jnp.sum(jnp.where(chosen, weight_grad[:, :, None], 0.0), axis=1)
        )
    logit_grad = (
        router_prob * (prob_grad - jnp.sum(router_prob * prob_grad, axis=-1, keepdims=True))
    ).astype(BF16)
    router_wgrad = matmul_tn(logit_grad, normed_rows)
    mid_grad = back_rows + matmul(logit_grad, router_t)
    mixer_wgrad = jnp.sum(mid_grad * hat_mid, axis=0)
    hidden_grad = own(cotangent).astype(F32) + norm_back(mid_grad, hat_mid, inverse_mid, gainmid_f)
    hidden_low = spread_gather(hidden_grad.astype(BF16), "col")

    out_cols = hidden_cols.astype(F32) + spread_sum(out_sum, "col", 1)
    if not dense:
        out_cols = out_cols + routed_own
    layer_out = out_cols.astype(BF16)

    attended_grad = matmul_nt(hidden_low, output_full).astype(BF16).reshape(tok_rows, heads_dev, VDIM)
    prob_wgrad = jnp.einsum(
        "thd,shd->hts", attended_grad, value_rows, preferred_element_type=F32
    )
    score_grad = (
        probs * (prob_wgrad - jnp.sum(probs * prob_wgrad, axis=-1, keepdims=True))
    ).astype(BF16)
    value_grad = jnp.einsum(
        "hts,thd->shd", probs_low, attended_grad, preferred_element_type=F32
    )
    query_grad_full = (
        jnp.einsum("hts,shd->thd", score_grad, keys_full, preferred_element_type=F32) * scale
    )
    key_grad = jnp.einsum("hts,thd->shd", score_grad, queries, preferred_element_type=F32)
    query_raw_grad = (
        jnp.concatenate(
            [
                query_grad_full[..., :NOPE],
                rotary_back(query_grad_full[..., NOPE:], cosine[:, None], sine[:, None]),
            ],
            axis=-1,
        )
        .astype(BF16)
        .reshape(tok_rows, query_cols)
    )
    keyval_rows_grad = (
        jnp.concatenate([key_grad[..., :NOPE], value_grad], axis=-1)
        .astype(BF16)
        .reshape(tok_rows, heads_dev * (NOPE + VDIM))
    )
    latnorm_part = matmul_nt(keyval_rows_grad, keyval_full)
    rope_part = jnp.sum(key_grad[..., NOPE:], axis=1)
    lat_rows = spread_sum(jnp.concatenate([latnorm_part, rope_part], axis=1), "col")
    lat_sum = spread_gather(lat_rows.astype(BF16), "col").astype(F32)
    latnorm_grad, rope_grad = lat_sum[:, :RANK], lat_sum[:, RANK:]
    latgain_wgrad = jnp.sum(own(latnorm_grad * hat_lat), axis=0)
    latent_rows_grad = jnp.concatenate(
        [
            norm_back(latnorm_grad, hat_lat, inverse_lat, gainlat_f),
            rotary_back(rope_grad, cosine, sine),
        ],
        axis=-1,
    ).astype(BF16)
    latent_own_grad = lax.dynamic_slice_in_dim(
        latent_rows_grad, col_index * latent_cols, latent_cols, 1
    )
    in_cols_grad = jnp.concatenate([query_raw_grad, latent_own_grad], axis=1)
    in_part = matmul(in_cols_grad, in_t)
    gainin_wgrad = jnp.sum(in_part * hat_in, axis=0)
    in_rows = spread_sum(in_part, "col")
    token_rows = hidden_grad + norm_back(in_rows, own(hat_in), own(inverse_in), gainin_f)
    tokens_grad = spread_gather(token_rows.astype(BF16), "col").astype(F32)

    output_grad = reduce(matmul_tn(attended, hidden_low), 1)
    keyval_grad = reduce(matmul_tn(latent_norm, keyval_rows_grad), 0)
    in_wgrad = reduce(matmul_tn(in_cols_grad, normed_in), 1)
    sums = shared_wgrad, output_grad, keyval_grad, in_wgrad
    sums, _ = lax.optimization_barrier((sums, token_rows))
    shared_wgrad, output_grad, keyval_grad, in_wgrad = (v.astype(F32) for v in sums)
    index = lax.axis_index(BLOCKS)
    piece = lambda v, size: lax.dynamic_slice_in_dim(v, index * size, size, v.ndim - 1)
    early = total(
        jnp.concatenate(
            [
                router_wgrad,
                mixer_wgrad[None],
                jnp.pad(latgain_wgrad, (0, width - RANK))[None],
                gainin_wgrad[None],
            ],
            axis=0,
        )
    )
    router_grad = piece(early[:experts_all], attn_gain.size).T
    mixer_gain_grad = piece(early[experts_all], mixer_gain.size)
    latent_gain_grad = piece(early[experts_all + 1], latent_gain.size)
    attn_gain_grad = piece(early[experts_all + 2], attn_gain.size)
    return (
        layer_out,
        tokens_grad,
        attn_gain_grad,
        in_wgrad[:query_cols].T,
        in_wgrad[query_cols:].T,
        latent_gain_grad,
        keyval_grad,
        output_grad,
        mixer_gain_grad,
        router_grad,
        shared_wgrad[:hidden_sh].T,
        shared_wgrad[hidden_sh : 2 * hidden_sh].T,
        shared_wgrad[2 * hidden_sh :],
        *expert_grads,
    )


def solution(mesh):
    rows, cols = P(BLOCKS, None), P(BLOCKS, "col")
    vector, turned = P(BLOCKS), P("col", BLOCKS)
    tall, flat = P(BLOCKS, None, "col"), P(BLOCKS, "col", None)
    in_specs = (
        rows, vector, cols, cols, vector, cols, turned, vector, rows, cols, cols, turned,
        tall, tall, flat, rows, rows, rows,
    )
    out_specs = (
        cols, rows, vector, cols, cols, vector, cols, turned, vector, rows, cols, cols, turned,
        tall, tall, flat,
    )
    return jax.shard_map(layer, mesh=mesh, in_specs=in_specs, out_specs=out_specs, check_vma=False)
```
